32 devices in a mesh: lat: 8 (over y, x, core), lon: 4 (over z).
Axes of the slice: x: 2, y: 2, z: 4, core: 2. Of those that a mesh axis runs over, the one named last changes fastest.
Arguments:
- tracers: float32 [4, 4, 256, 720], P(None, None, 'lat', 'lon'), may hold values from -6 to 6
- courant: float32 [2, 4, 256, 720], P(None, None, 'lat', 'lon'), may hold values from -0.8 to 0.8
- cutoffs: int32 [256], replicated, may hold values from 1 to 360, as said below
Outputs:
- updated: float32 [4, 4, 256, 720], P(None, None, 'lat', 'lon')
- filtered_zonal: float32 [4, 256, 720], P(None, 'lat', 'lon')
The draws below stay inside these ranges and needn't reach their ends.
Inputs may be any that keep to these rules, and one draw needn't show every extreme that they name: cutoffs[j] is 360 for every row j with min(j, 255 - j) >= 64, below 360 for all other rows, and 1 at the two pole rows.
All inputs are finite; a program needn't handle non-finite values.
Results may differ from the reference program's by a relative error of at most 0.0003.
Values sent between devices are 32-bit elements; how exact they have to be, the bound alone decides.
A program may use at most 64 MiB of HBM per device.

```python
import math
import jax
import jax.numpy as jnp
from jax import lax

LEV = 4
TRAC = 4
NLAT = 256
NLON = 720


def draw_cutoffs(key, part):
    row_ids = jnp.arange(NLAT, dtype=jnp.int32)
    distance = jnp.minimum(row_ids, NLAT - 1 - row_ids)
    polar_band = NLAT // 4
    jitter = jax.random.randint(key, (NLAT,), -3, 4, dtype=jnp.int32)
    ramped = 1 + distance * (NLON // 2 - 2) // polar_band + jitter
    ramped = jnp.clip(ramped, 1, NLON // 2 - 1)
    ramped = jnp.where(distance == 0, 1, ramped)
    return jnp.where(distance < polar_band, ramped, NLON // 2).astype(jnp.int32)


def level_of(key, extent, cuts, least, top_value):
    def one(position, shards_of):
        steps = jax.random.uniform(jax.random.fold_in(jax.random.fold_in(key, 6), position), (shards_of,), jnp.float32, least / len(cuts), top_value / len(cuts))
        return jnp.repeat(jnp.exp(steps), extent[position] // shards_of).reshape((-1,) + (1,) * (len(extent) - position - 1))

    gain = one(*cuts[0])
    for cut in cuts[1:]:
        gain = gain * one(*cut)
    return gain


def bell_draw(rng, shape, width, most, shards=(), kind=jnp.bfloat16):
    factor_of = level_of(rng, shape, shards, -0.22, 0.18) if shards else 1.0
    array = jax.random.normal(rng, shape, jnp.float32) * width * factor_of
    return jnp.minimum(jnp.maximum(array, -most), most).astype(kind)


def setup_inputs(seed: int = 0) -> dict:
    arg_keys = jax.random.split(jax.random.key(seed), 4)
    return {
        "tracers": bell_draw(arg_keys[0], (LEV, TRAC, NLAT, NLON), 1.0, 6.0, ((2, 8), (3, 4)), jnp.float32),
        "courant": jnp.clip(jax.random.uniform(arg_keys[1], (2, LEV, NLAT, NLON), jnp.float32, -0.8, 0.8) * level_of(arg_keys[1], (2, LEV, NLAT, NLON), ((2, 8), (3, 4)), -0.4, 0.0), -0.8, 0.8),
        "cutoffs": draw_cutoffs(jax.random.fold_in(arg_keys[3], 71), 0),
    }


def take_range(values, start, count, axis_index):
    return lax.slice_in_dim(values, start, start + count, axis=axis_index)


def ppm_flux(extended, courant_faces, axis_index):
    cell_count = extended.shape[axis_index] - 6
    edge_values = (7.0 / 12.0) * (take_range(extended, 1, cell_count + 3, axis_index) + take_range(extended, 2, cell_count + 3, axis_index)) - (1.0 / 12.0) * (take_range(extended, 0, cell_count + 3, axis_index) + take_range(extended, 3, cell_count + 3, axis_index))
    left_edge = take_range(edge_values, 0, cell_count + 2, axis_index)
    right_edge = take_range(edge_values, 1, cell_count + 2, axis_index)
    centre = take_range(extended, 2, cell_count + 2, axis_index)
    slopes = right_edge - left_edge
    curvature = 6.0 * centre - 3.0 * (left_edge + right_edge)
    upwind = take_range(right_edge, 0, cell_count + 1, axis_index) - 0.5 * courant_faces * (take_range(slopes, 0, cell_count + 1, axis_index) - (1.0 - courant_faces * (2.0 / 3.0)) * take_range(curvature, 0, cell_count + 1, axis_index))
    downwind = take_range(left_edge, 1, cell_count + 1, axis_index) - 0.5 * courant_faces * (take_range(slopes, 1, cell_count + 1, axis_index) + (1.0 + courant_faces * (2.0 / 3.0)) * take_range(curvature, 1, cell_count + 1, axis_index))
    return courant_faces * jnp.where(courant_faces > 0, upwind, downwind)


def metric_weights(first_row, row_count, grid_rows):
    faces = first_row + jnp.arange(-1, row_count, dtype=jnp.int32)
    centres = first_row + jnp.arange(row_count, dtype=jnp.int32)
    face_weight = jnp.sin(jnp.minimum(faces + 1, grid_rows - 1 - faces).astype(jnp.float32) * (math.pi / grid_rows))
    cell_weight = jnp.sin((jnp.minimum(centres, grid_rows - 1 - centres).astype(jnp.float32) + 0.5) * (math.pi / grid_rows))
    return face_weight, cell_weight


def reference(tracers, courant, cutoffs):
    zonal = courant[0]
    meridional = courant[1]
    spectrum = jnp.fft.rfft(zonal, axis=2)
    waves = jnp.arange(NLON // 2 + 1, dtype=jnp.int32)
    keep_mask = waves[None, None, :] <= cutoffs[None, :, None]
    lowpass = jnp.fft.irfft(jnp.where(keep_mask, spectrum, 0.0), n=NLON, axis=2).astype(jnp.float32)
    filtered_zonal = jnp.where((cutoffs < NLON // 2)[None, :, None], lowpass, zonal)
    face_weight, cell_weight = metric_weights(jnp.int32(0), NLAT, NLAT)

    def one_level(items):
        level_tracers, zonal_level, merid_level = items
        lon_ext = jnp.concatenate([level_tracers[:, :, -3:], level_tracers, level_tracers[:, :, :3]], axis=2)
        zonal_faces = jnp.concatenate([zonal_level[:, -1:], zonal_level], axis=1)[None]
        flux_east = ppm_flux(lon_ext, zonal_faces, 2)
        lat_ext = jnp.pad(level_tracers, ((0, 0), (3, 3), (0, 0)))
        merid_faces = jnp.pad(merid_level, ((1, 0), (0, 0)))[None]
        flux_north = ppm_flux(lat_ext, merid_faces, 1) * face_weight[None, :, None]
        change = (flux_east[:, :, 1:] - flux_east[:, :, :-1]) + (flux_north[:, 1:, :] - flux_north[:, :-1, :]) / cell_weight[None, :, None]
        return level_tracers - change

    updated = lax.map(one_level, (tracers, filtered_zonal, meridional))
    return updated, filtered_zonal
```

```python
import math

import jax
import numpy as np
import jax.numpy as jnp
from jax import lax
from jax.sharding import PartitionSpec as P


def padded(cells, sides, width, closed):
    for axis, dim in sides:
        count = lax.axis_size(axis)
        ends = count if closed else count - 1
        head = lax.slice_in_dim(cells, 0, width, axis=dim)
        tail = lax.slice_in_dim(cells, cells.shape[dim] - width, cells.shape[dim], axis=dim)
        cells = jnp.concatenate(
            [
                lax.ppermute(tail, axis, [(i, (i + 1) % count) for i in range(ends)]),
                cells,
                lax.ppermute(head, axis, [((i + 1) % count, i) for i in range(ends)]),
            ],
            axis=dim,
        )
    return cells


def take_range(values, start, count, axis_index):
    return lax.slice_in_dim(values, start, start + count, axis=axis_index)


def ppm_flux(extended, courant_faces, axis_index):
    cell_count = extended.shape[axis_index] - 6
    edge_values = 7.0 / 12.0 * (
        take_range(extended, 1, cell_count + 3, axis_index)
        + take_range(extended, 2, cell_count + 3, axis_index)
    ) - 1.0 / 12.0 * (
        take_range(extended, 0, cell_count + 3, axis_index)
        + take_range(extended, 3, cell_count + 3, axis_index)
    )
    left_edge = take_range(edge_values, 0, cell_count + 2, axis_index)
    right_edge = take_range(edge_values, 1, cell_count + 2, axis_index)
    centre = take_range(extended, 2, cell_count + 2, axis_index)
    slopes = right_edge - left_edge
    curvature = 6.0 * centre - 3.0 * (left_edge + right_edge)
    upwind = take_range(right_edge, 0, cell_count + 1, axis_index) - 0.5 * courant_faces * (
        take_range(slopes, 0, cell_count + 1, axis_index)
        - (1.0 - courant_faces * (2.0 / 3.0)) * take_range(curvature, 0, cell_count + 1, axis_index)
    )
    downwind = take_range(left_edge, 1, cell_count + 1, axis_index) - 0.5 * courant_faces * (
        take_range(slopes, 1, cell_count + 1, axis_index)
        + (1.0 + courant_faces * (2.0 / 3.0)) * take_range(curvature, 1, cell_count + 1, axis_index)
    )
    return courant_faces * jnp.where(courant_faces > 0, upwind, downwind)


def metric_weights(first_row, row_count, grid_rows):
    faces = first_row + jnp.arange(-1, row_count, dtype=jnp.int32)
    centres = first_row + jnp.arange(row_count, dtype=jnp.int32)
    face_weight = jnp.sin(
        jnp.minimum(faces + 1, grid_rows - 1 - faces).astype(jnp.float32) * (math.pi / grid_rows)
    )
    cell_weight = jnp.sin(
        (jnp.minimum(centres, grid_rows - 1 - centres).astype(jnp.float32) + 0.5)
        * (math.pi / grid_rows)
    )
    return (face_weight, cell_weight)


def angle_table(first_ids, second_ids, period):
    product = first_ids[:, None] * second_ids[None, :] % period
    angles = product.astype(jnp.float32) * (2.0 * math.pi / period)
    return (jnp.cos(angles), jnp.sin(angles))


def spectral_lowpass(row_block, limits, outer_count):
    row_count, circle = row_block.shape
    inner_count = circle // outer_count
    highest = lax.Precision.HIGHEST
    grid_values = row_block.reshape(row_count, outer_count, inner_count)
    outer_ids = jnp.arange(outer_count, dtype=jnp.int32)
    inner_ids = jnp.arange(inner_count, dtype=jnp.int32)
    outer_cos, outer_sin = angle_table(outer_ids, outer_ids, outer_count)
    inner_cos, inner_sin = angle_table(inner_ids, inner_ids, inner_count)
    twiddle_cos, twiddle_sin = angle_table(inner_ids, outer_ids, circle)
    first_real = jnp.einsum("rab,ak->rbk", grid_values, outer_cos, precision=highest)
    first_imag = -jnp.einsum("rab,ak->rbk", grid_values, outer_sin, precision=highest)
    turned_real = first_real * twiddle_cos + first_imag * twiddle_sin
    turned_imag = first_imag * twiddle_cos - first_real * twiddle_sin
    coeff_real = jnp.einsum("rbk,bj->rjk", turned_real, inner_cos, precision=highest) + jnp.einsum(
        "rbk,bj->rjk", turned_imag, inner_sin, precision=highest
    )
    coeff_imag = jnp.einsum("rbk,bj->rjk", turned_imag, inner_cos, precision=highest) - jnp.einsum(
        "rbk,bj->rjk", turned_real, inner_sin, precision=highest
    )
    wavenumber = inner_ids[:, None] * outer_count + outer_ids[None, :]
    folded = jnp.minimum(wavenumber, circle - wavenumber)
    keep_mask = folded[None, :, :] <= limits[:, None, None]
    coeff_real = jnp.where(keep_mask, coeff_real, 0.0)
    coeff_imag = jnp.where(keep_mask, coeff_imag, 0.0)
    back_real = jnp.einsum("rjk,jb->rbk", coeff_real, inner_cos, precision=highest) - jnp.einsum(
        "rjk,jb->rbk", coeff_imag, inner_sin, precision=highest
    )
    back_imag = jnp.einsum("rjk,jb->rbk", coeff_imag, inner_cos, precision=highest) + jnp.einsum(
        "rjk,jb->rbk", coeff_real, inner_sin, precision=highest
    )
    reverted_real = back_real * twiddle_cos - back_imag * twiddle_sin
    reverted_imag = back_imag * twiddle_cos + back_real * twiddle_sin
    signal = jnp.einsum("rbk,ka->rab", reverted_real, outer_cos, precision=highest) - jnp.einsum(
        "rbk,ka->rab", reverted_imag, outer_sin, precision=highest
    )
    return (signal / circle).reshape(row_count, circle)


def dense_tables(circle):
    half = circle // 2
    cell_ids = np.arange(circle, dtype=np.int64)
    cos_ids = np.arange(half + 1, dtype=np.int64)
    sin_ids = np.arange(1, half, dtype=np.int64)
    forward = np.concatenate(
        [
            np.cos(2.0 * np.pi * ((cell_ids[:, None] * cos_ids[None, :]) % circle) / circle),
            np.sin(2.0 * np.pi * ((cell_ids[:, None] * sin_ids[None, :]) % circle) / circle),
        ],
        axis=1,
    )
    out_ids = np.arange(-1, circle, dtype=np.int64)
    cos_scale = np.where((cos_ids == 0) | (cos_ids == half), 1.0, 2.0) / circle
    inverse = np.concatenate(
        [
            cos_scale[:, None]
            * np.cos(2.0 * np.pi * ((cos_ids[:, None] * out_ids[None, :]) % circle) / circle),
            (2.0 / circle)
            * np.sin(2.0 * np.pi * ((sin_ids[:, None] * out_ids[None, :]) % circle) / circle),
        ],
        axis=0,
    )
    wavenumber = np.concatenate([cos_ids, sin_ids]).astype(np.int32)
    return (
        jnp.asarray(forward.astype(np.float32)),
        jnp.asarray(inverse.astype(np.float32)),
        jnp.asarray(wavenumber),
    )


def dense_lowpass(row_block, limits):
    circle = row_block.shape[1]
    forward, inverse, wavenumber = dense_tables(circle)
    highest = lax.Precision.HIGHEST
    coeff = jnp.dot(row_block, forward, precision=highest)
    coeff = jnp.where(wavenumber[None, :] <= limits[:, None], coeff, 0.0)
    return jnp.dot(coeff, inverse, precision=highest)


def circle_filter(row_block, limits, lon_groups):
    row_count, block_cols = row_block.shape
    whole_rows = lax.all_to_all(row_block, "lon", split_axis=0, concat_axis=1, tiled=True)
    circle = whole_rows.shape[1]
    held_count = row_count // lon_groups
    row_limits = lax.dynamic_slice_in_dim(limits, lax.axis_index("lon") * held_count, held_count)
    whole_ext = jnp.concatenate([whole_rows[:, -1:], whole_rows], axis=1)
    if circle <= 2048:
        lowpass_ext = dense_lowpass(whole_rows, row_limits)
    else:
        lowpass = spectral_lowpass(whole_rows, row_limits, lon_groups)
        lowpass_ext = jnp.concatenate([lowpass[:, -1:], lowpass], axis=1)
    lowpass_ext = jnp.where((row_limits < circle // 2)[:, None], lowpass_ext, whole_ext)
    slabs = jnp.stack(
        [lowpass_ext[:, k * block_cols : (k + 1) * block_cols + 1] for k in range(lon_groups)],
        axis=0,
    )
    back = lax.all_to_all(slabs, "lon", split_axis=0, concat_axis=1, tiled=True)
    return back.reshape(row_count, block_cols + 1)


def body(tracers, courant, cutoffs):
    levels, tracer_count, lat_rows, lon_cols = tracers.shape
    lon_groups = lax.axis_size("lon")
    lat_bands = lax.axis_size("lat")
    band_index = lax.axis_index("lat")
    grid_rows = lat_rows * lat_bands
    zonal = courant[0]
    meridional = courant[1]
    lat_stack = jnp.concatenate([tracers, meridional[:, None]], axis=1)
    lat_ext = padded(lat_stack, (("lat", 2),), 3, False)
    lon_ext = padded(tracers, (("lon", 3),), 3, True)
    flat_count = levels * lat_rows
    flat_zonal = zonal.reshape(flat_count, lon_cols)
    local_limits = lax.dynamic_slice_in_dim(cutoffs, band_index * lat_rows, lat_rows)
    filtered_flat = circle_filter(flat_zonal, jnp.tile(local_limits, levels), lon_groups)
    zonal_faces = filtered_flat.reshape(levels, 1, lat_rows, lon_cols + 1)
    filtered_zonal = zonal_faces[:, 0, :, 1:]
    flux_east = ppm_flux(lon_ext, zonal_faces, 3)
    face_weight, cell_weight = metric_weights(band_index * lat_rows, lat_rows, grid_rows)
    flux_north = (
        ppm_flux(lat_ext[:, :tracer_count], lat_ext[:, tracer_count:, 2 : lat_rows + 3, :], 2)
        * face_weight[None, None, :, None]
    )
    change = (
        flux_east[:, :, :, 1:]
        - flux_east[:, :, :, :-1]
        + (flux_north[:, :, 1:, :] - flux_north[:, :, :-1, :]) / cell_weight[None, None, :, None]
    )
    return (tracers - change, filtered_zonal)


def solution(mesh):
    in_specs = (P(None, None, "lat", "lon"), P(None, None, "lat", "lon"), P())
    out_specs = (P(None, None, "lat", "lon"), P(None, "lat", "lon"))
    return jax.shard_map(body, mesh=mesh, in_specs=in_specs, out_specs=out_specs, check_vma=False)
```

```python
import math

import jax
import numpy as np
import jax.numpy as jnp
from jax import lax
from jax.sharding import PartitionSpec as P


def padded(cells, sides, width, closed):
    for axis, dim in sides:
        count = lax.axis_size(axis)
        ends = count if closed else count - 1
        head = lax.slice_in_dim(cells, 0, width, axis=dim)
        tail = lax.slice_in_dim(cells, cells.shape[dim] - width, cells.shape[dim], axis=dim)
        cells = jnp.concatenate(
            [
                lax.ppermute(tail, axis, [(i, (i + 1) % count) for i in range(ends)]),
                cells,
                lax.ppermute(head, axis, [((i + 1) % count, i) for i in range(ends)]),
            ],
            axis=dim,
        )
    return cells


def take_range(values, start, count, axis_index):
    return lax.slice_in_dim(values, start, start + count, axis=axis_index)


def ppm_flux(extended, courant_faces, axis_index):
    cell_count = extended.shape[axis_index] - 6
    edge_values = 7.0 / 12.0 * (
        take_range(extended, 1, cell_count + 3, axis_index)
        + take_range(extended, 2, cell_count + 3, axis_index)
    ) - 1.0 / 12.0 * (
        take_range(extended, 0, cell_count + 3, axis_index)
        + take_range(extended, 3, cell_count + 3, axis_index)
    )
    left_edge = take_range(edge_values, 0, cell_count + 2, axis_index)
    right_edge = take_range(edge_values, 1, cell_count + 2, axis_index)
    centre = take_range(extended, 2, cell_count + 2, axis_index)
    slopes = right_edge - left_edge
    curvature = 6.0 * centre - 3.0 * (left_edge + right_edge)
    upwind = take_range(right_edge, 0, cell_count + 1, axis_index) - 0.5 * courant_faces * (
        take_range(slopes, 0, cell_count + 1, axis_index)
        - (1.0 - courant_faces * (2.0 / 3.0)) * take_range(curvature, 0, cell_count + 1, axis_index)
    )
    downwind = take_range(left_edge, 1, cell_count + 1, axis_index) - 0.5 * courant_faces * (
        take_range(slopes, 1, cell_count + 1, axis_index)
        + (1.0 + courant_faces * (2.0 / 3.0)) * take_range(curvature, 1, cell_count + 1, axis_index)
    )
    return courant_faces * jnp.where(courant_faces > 0, upwind, downwind)


def metric_weights(first_row, row_count, grid_rows):
    faces = first_row + jnp.arange(-1, row_count, dtype=jnp.int32)
    centres = first_row + jnp.arange(row_count, dtype=jnp.int32)
    face_weight = jnp.sin(
        jnp.minimum(faces + 1, grid_rows - 1 - faces).astype(jnp.float32) * (math.pi / grid_rows)
    )
    cell_weight = jnp.sin(
        (jnp.minimum(centres, grid_rows - 1 - centres).astype(jnp.float32) + 0.5)
        * (math.pi / grid_rows)
    )
    return (face_weight, cell_weight)


def angle_table(first_ids, second_ids, period):
    product = first_ids[:, None] * second_ids[None, :] % period
    angles = product.astype(jnp.float32) * (2.0 * math.pi / period)
    return (jnp.cos(angles), jnp.sin(angles))


def spectral_lowpass(row_block, limits, outer_count):
    row_count, circle = row_block.shape
    inner_count = circle // outer_count
    highest = lax.Precision.HIGHEST
    grid_values = row_block.reshape(row_count, outer_count, inner_count)
    outer_ids = jnp.arange(outer_count, dtype=jnp.int32)
    inner_ids = jnp.arange(inner_count, dtype=jnp.int32)
    outer_cos, outer_sin = angle_table(outer_ids, outer_ids, outer_count)
    inner_cos, inner_sin = angle_table(inner_ids, inner_ids, inner_count)
    twiddle_cos, twiddle_sin = angle_table(inner_ids, outer_ids, circle)
    first_real = jnp.einsum("rab,ak->rbk", grid_values, outer_cos, precision=highest)
    first_imag = -jnp.einsum("rab,ak->rbk", grid_values, outer_sin, precision=highest)
    turned_real = first_real * twiddle_cos + first_imag * twiddle_sin
    turned_imag = first_imag * twiddle_cos - first_real * twiddle_sin
    coeff_real = jnp.einsum("rbk,bj->rjk", turned_real, inner_cos, precision=highest) + jnp.einsum(
        "rbk,bj->rjk", turned_imag, inner_sin, precision=highest
    )
    coeff_imag = jnp.einsum("rbk,bj->rjk", turned_imag, inner_cos, precision=highest) - jnp.einsum(
        "rbk,bj->rjk", turned_real, inner_sin, precision=highest
    )
    wavenumber = inner_ids[:, None] * outer_count + outer_ids[None, :]
    folded = jnp.minimum(wavenumber, circle - wavenumber)
    keep_mask = folded[None, :, :] <= limits[:, None, None]
    coeff_real = jnp.where(keep_mask, coeff_real, 0.0)
    coeff_imag = jnp.where(keep_mask, coeff_imag, 0.0)
    back_real = jnp.einsum("rjk,jb->rbk", coeff_real, inner_cos, precision=highest) - jnp.einsum(
        "rjk,jb->rbk", coeff_imag, inner_sin, precision=highest
    )
    back_imag = jnp.einsum("rjk,jb->rbk", coeff_imag, inner_cos, precision=highest) + jnp.einsum(
        "rjk,jb->rbk", coeff_real, inner_sin, precision=highest
    )
    reverted_real = back_real * twiddle_cos - back_imag * twiddle_sin
    reverted_imag = back_imag * twiddle_cos + back_real * twiddle_sin
    signal = jnp.einsum("rbk,ka->rab", reverted_real, outer_cos, precision=highest) - jnp.einsum(
        "rbk,ka->rab", reverted_imag, outer_sin, precision=highest
    )
    return (signal / circle).reshape(row_count, circle)


def dense_tables(circle):
    half = circle // 2
    cell_ids = np.arange(-1, circle, dtype=np.int64)
    cos_ids = np.arange(half + 1, dtype=np.int64)
    sin_ids = np.arange(1, half, dtype=np.int64)
    table = np.concatenate(
        [
            np.cos(2.0 * np.pi * ((cell_ids[:, None] * cos_ids[None, :]) % circle) / circle),
            np.sin(2.0 * np.pi * ((cell_ids[:, None] * sin_ids[None, :]) % circle) / circle),
        ],
        axis=1,
    )
    wavenumber = np.concatenate([cos_ids, sin_ids])
    scale = np.where((wavenumber == 0) | (wavenumber == half), 1.0, 2.0) / circle
    return (
        jnp.asarray(table.astype(np.float32)),
        jnp.asarray(scale.astype(np.float32)),
        jnp.asarray(wavenumber.astype(np.int32)),
    )


def body(tracers, courant, cutoffs):
    levels, tracer_count, lat_rows, lon_cols = tracers.shape
    lon_groups = lax.axis_size("lon")
    lon_index = lax.axis_index("lon")
    lat_bands = lax.axis_size("lat")
    band_index = lax.axis_index("lat")
    grid_rows = lat_rows * lat_bands
    zonal = courant[0]
    meridional = courant[1]
    lat_stack = jnp.concatenate([tracers, meridional[:, None]], axis=1)
    lat_ext = padded(lat_stack, (("lat", 2),), 3, False)
    flat_count = levels * lat_rows
    flat_zonal = zonal.reshape(flat_count, lon_cols)
    edges = jnp.concatenate([tracers[..., :3], tracers[..., lon_cols - 3 :]], axis=-1)
    gathered = lax.all_gather(flat_zonal, "lon", axis=0)
    gathered_edges = lax.all_gather(edges, "lon", axis=0)
    west_index = (lon_index + lon_groups - 1) % lon_groups
    east_index = (lon_index + 1) % lon_groups
    west = lax.dynamic_index_in_dim(gathered_edges, west_index, 0, keepdims=False)[..., 3:]
    east = lax.dynamic_index_in_dim(gathered_edges, east_index, 0, keepdims=False)[..., :3]
    lon_ext = jnp.concatenate([west, tracers, east], axis=-1)
    local_limits = lax.dynamic_slice_in_dim(cutoffs, band_index * lat_rows, lat_rows)
    limits = jnp.tile(local_limits, levels)
    circle = lon_cols * lon_groups
    west_raw = lax.dynamic_index_in_dim(gathered, west_index, 0, keepdims=False)[:, -1:]
    raw_ext = jnp.concatenate([west_raw, flat_zonal], axis=1)
    if circle <= 2048:
        table, scale, wavenumber = dense_tables(circle)
        high = lax.Precision.HIGH
        coeff = jnp.einsum(
            "prm,pmw->rw",
            gathered,
            table[1:].reshape(lon_groups, lon_cols, circle),
            precision=high,
        )
        coeff = jnp.where(wavenumber[None, :] <= limits[:, None], coeff * scale[None, :], 0.0)
        local_table = lax.dynamic_slice_in_dim(table, lon_index * lon_cols, lon_cols + 1, axis=0)
        lowpass_ext = jnp.einsum("rw,nw->rn", coeff, local_table, precision=high)
    else:
        whole_rows = jnp.transpose(gathered, (1, 0, 2)).reshape(flat_count, circle)
        lowpass = spectral_lowpass(whole_rows, limits, lon_groups)
        lowpass = jnp.concatenate([lowpass[:, -1:], lowpass], axis=1)
        lowpass_ext = lax.dynamic_slice_in_dim(lowpass, lon_index * lon_cols, lon_cols + 1, axis=1)
    filtered_flat = jnp.where((limits < circle // 2)[:, None], lowpass_ext, raw_ext)
    zonal_faces = filtered_flat.reshape(levels, 1, lat_rows, lon_cols + 1)
    filtered_zonal = zonal_faces[:, 0, :, 1:]
    flux_east = ppm_flux(lon_ext, zonal_faces, 3)
    face_weight, cell_weight = metric_weights(band_index * lat_rows, lat_rows, grid_rows)
    flux_north = (
        ppm_flux(lat_ext[:, :tracer_count], lat_ext[:, tracer_count:, 2 : lat_rows + 3, :], 2)
        * face_weight[None, None, :, None]
    )
    change = (
        flux_east[:, :, :, 1:]
        - flux_east[:, :, :, :-1]
        + (flux_north[:, :, 1:, :] - flux_north[:, :, :-1, :]) / cell_weight[None, None, :, None]
    )
    return (tracers - change, filtered_zonal)


def solution(mesh):
    in_specs = (P(None, None, "lat", "lon"), P(None, None, "lat", "lon"), P())
    out_specs = (P(None, None, "lat", "lon"), P(None, "lat", "lon"))
    return jax.shard_map(body, mesh=mesh, in_specs=in_specs, out_specs=out_specs, check_vma=False)
```

```python
import math

import jax
import numpy as np
import jax.numpy as jnp
from jax import lax
from jax.sharding import PartitionSpec as P


def padded(cells, sides, width, closed):
    for axis, dim in sides:
        count = lax.axis_size(axis)
        ends = count if closed else count - 1
        head = lax.slice_in_dim(cells, 0, width, axis=dim)
        tail = lax.slice_in_dim(cells, cells.shape[dim] - width, cells.shape[dim], axis=dim)
        cells = jnp.concatenate(
            [
                lax.ppermute(tail, axis, [(i, (i + 1) % count) for i in range(ends)]),
                cells,
                lax.ppermute(head, axis, [((i + 1) % count, i) for i in range(ends)]),
            ],
            axis=dim,
        )
    return cells


def take_range(values, start, count, axis_index):
    return lax.slice_in_dim(values, start, start + count, axis=axis_index)


def ppm_flux(extended, courant_faces, axis_index):
    cell_count = extended.shape[axis_index] - 6
    edge_values = 7.0 / 12.0 * (
        take_range(extended, 1, cell_count + 3, axis_index)
        + take_range(extended, 2, cell_count + 3, axis_index)
    ) - 1.0 / 12.0 * (
        take_range(extended, 0, cell_count + 3, axis_index)
        + take_range(extended, 3, cell_count + 3, axis_index)
    )
    left_edge = take_range(edge_values, 0, cell_count + 2, axis_index)
    right_edge = take_range(edge_values, 1, cell_count + 2, axis_index)
    centre = take_range(extended, 2, cell_count + 2, axis_index)
    slopes = right_edge - left_edge
    curvature = 6.0 * centre - 3.0 * (left_edge + right_edge)
    upwind = take_range(right_edge, 0, cell_count + 1, axis_index) - 0.5 * courant_faces * (
        take_range(slopes, 0, cell_count + 1, axis_index)
        - (1.0 - courant_faces * (2.0 / 3.0)) * take_range(curvature, 0, cell_count + 1, axis_index)
    )
    downwind = take_range(left_edge, 1, cell_count + 1, axis_index) - 0.5 * courant_faces * (
        take_range(slopes, 1, cell_count + 1, axis_index)
        + (1.0 + courant_faces * (2.0 / 3.0)) * take_range(curvature, 1, cell_count + 1, axis_index)
    )
    return courant_faces * jnp.where(courant_faces > 0, upwind, downwind)


def metric_weights(first_row, row_count, grid_rows):
    faces = first_row + jnp.arange(-1, row_count, dtype=jnp.int32)
    centres = first_row + jnp.arange(row_count, dtype=jnp.int32)
    face_weight = jnp.sin(
        jnp.minimum(faces + 1, grid_rows - 1 - faces).astype(jnp.float32) * (math.pi / grid_rows)
    )
    cell_weight = jnp.sin(
        (jnp.minimum(centres, grid_rows - 1 - centres).astype(jnp.float32) + 0.5)
        * (math.pi / grid_rows)
    )
    return (face_weight, cell_weight)


def angle_table(first_ids, second_ids, period):
    product = first_ids[:, None] * second_ids[None, :] % period
    angles = product.astype(jnp.float32) * (2.0 * math.pi / period)
    return (jnp.cos(angles), jnp.sin(angles))


def spectral_lowpass(row_block, limits, outer_count):
    row_count, circle = row_block.shape
    inner_count = circle // outer_count
    highest = lax.Precision.HIGHEST
    grid_values = row_block.reshape(row_count, outer_count, inner_count)
    outer_ids = jnp.arange(outer_count, dtype=jnp.int32)
    inner_ids = jnp.arange(inner_count, dtype=jnp.int32)
    outer_cos, outer_sin = angle_table(outer_ids, outer_ids, outer_count)
    inner_cos, inner_sin = angle_table(inner_ids, inner_ids, inner_count)
    twiddle_cos, twiddle_sin = angle_table(inner_ids, outer_ids, circle)
    first_real = jnp.einsum("rab,ak->rbk", grid_values, outer_cos, precision=highest)
    first_imag = -jnp.einsum("rab,ak->rbk", grid_values, outer_sin, precision=highest)
    turned_real = first_real * twiddle_cos + first_imag * twiddle_sin
    turned_imag = first_imag * twiddle_cos - first_real * twiddle_sin
    coeff_real = jnp.einsum("rbk,bj->rjk", turned_real, inner_cos, precision=highest) + jnp.einsum(
        "rbk,bj->rjk", turned_imag, inner_sin, precision=highest
    )
    coeff_imag = jnp.einsum("rbk,bj->rjk", turned_imag, inner_cos, precision=highest) - jnp.einsum(
        "rbk,bj->rjk", turned_real, inner_sin, precision=highest
    )
    wavenumber = inner_ids[:, None] * outer_count + outer_ids[None, :]
    folded = jnp.minimum(wavenumber, circle - wavenumber)
    keep_mask = folded[None, :, :] <= limits[:, None, None]
    coeff_real = jnp.where(keep_mask, coeff_real, 0.0)
    coeff_imag = jnp.where(keep_mask, coeff_imag, 0.0)
    back_real = jnp.einsum("rjk,jb->rbk", coeff_real, inner_cos, precision=highest) - jnp.einsum(
        "rjk,jb->rbk", coeff_imag, inner_sin, precision=highest
    )
    back_imag = jnp.einsum("rjk,jb->rbk", coeff_imag, inner_cos, precision=highest) + jnp.einsum(
        "rjk,jb->rbk", coeff_real, inner_sin, precision=highest
    )
    reverted_real = back_real * twiddle_cos - back_imag * twiddle_sin
    reverted_imag = back_imag * twiddle_cos + back_real * twiddle_sin
    signal = jnp.einsum("rbk,ka->rab", reverted_real, outer_cos, precision=highest) - jnp.einsum(
        "rbk,ka->rab", reverted_imag, outer_sin, precision=highest
    )
    return (signal / circle).reshape(row_count, circle)


def dense_tables(circle):
    half = circle // 2
    cell_ids = np.arange(-1, circle, dtype=np.int64)
    cos_ids = np.arange(half + 1, dtype=np.int64)
    sin_ids = np.arange(1, half, dtype=np.int64)
    table = np.concatenate(
        [
            np.cos(2.0 * np.pi * ((cell_ids[:, None] * cos_ids[None, :]) % circle) / circle),
            np.sin(2.0 * np.pi * ((cell_ids[:, None] * sin_ids[None, :]) % circle) / circle),
        ],
        axis=1,
    )
    wavenumber = np.concatenate([cos_ids, sin_ids])
    scale = np.where((wavenumber == 0) | (wavenumber == half), 1.0, 2.0) / circle
    return (
        jnp.asarray(table.astype(np.float32)),
        jnp.asarray(scale.astype(np.float32)),
        jnp.asarray(wavenumber.astype(np.int32)),
    )


def body(tracers, courant, cutoffs):
    levels, tracer_count, lat_rows, lon_cols = tracers.shape
    lon_groups = lax.axis_size("lon")
    lon_index = lax.axis_index("lon")
    lat_bands = lax.axis_size("lat")
    band_index = lax.axis_index("lat")
    grid_rows = lat_rows * lat_bands
    zonal = courant[0]
    meridional = courant[1]
    lat_stack = jnp.concatenate([tracers, meridional[:, None]], axis=1)
    lat_ext = padded(lat_stack, (("lat", 2),), 3, False)
    flat_count = levels * lat_rows
    flat_zonal = zonal.reshape(flat_count, lon_cols)
    edges = jnp.concatenate([tracers[..., :3], tracers[..., lon_cols - 3 :]], axis=-1)
    west_index = (lon_index + lon_groups - 1) % lon_groups
    east_index = (lon_index + 1) % lon_groups
    if lon_groups <= 8:
        edge_rows = jnp.transpose(edges, (0, 2, 1, 3)).reshape(flat_count, tracer_count * 6)
        payload = jnp.concatenate([flat_zonal, edge_rows], axis=1)
        received = [payload] + [
            lax.ppermute(payload, "lon", [(i, (i + s) % lon_groups) for i in range(lon_groups)])
            for s in range(1, lon_groups)
        ]
        stacked = jnp.stack([part[:, :lon_cols] for part in received], axis=0)
        order = (lon_index - jnp.arange(lon_groups, dtype=jnp.int32)) % lon_groups
        gathered = jnp.take(stacked, order, axis=0)

        def edge_block(part):
            block = part[:, lon_cols:].reshape(levels, lat_rows, tracer_count, 6)
            return jnp.transpose(block, (0, 2, 1, 3))

        west = edge_block(received[1 % lon_groups])[..., 3:]
        east = edge_block(received[(lon_groups - 1) % lon_groups])[..., :3]
        west_raw = received[1 % lon_groups][:, lon_cols - 1 : lon_cols]
    else:
        gathered = lax.all_gather(flat_zonal, "lon", axis=0)
        gathered_edges = lax.all_gather(edges, "lon", axis=0)
        west = lax.dynamic_index_in_dim(gathered_edges, west_index, 0, keepdims=False)[..., 3:]
        east = lax.dynamic_index_in_dim(gathered_edges, east_index, 0, keepdims=False)[..., :3]
        west_raw = lax.dynamic_index_in_dim(gathered, west_index, 0, keepdims=False)[:, -1:]
    lon_ext = jnp.concatenate([west, tracers, east], axis=-1)
    local_limits = lax.dynamic_slice_in_dim(cutoffs, band_index * lat_rows, lat_rows)
    limits = jnp.tile(local_limits, levels)
    circle = lon_cols * lon_groups
    raw_ext = jnp.concatenate([west_raw, flat_zonal], axis=1)
    if circle <= 2048:
        table, scale, wavenumber = dense_tables(circle)
        high = lax.Precision.HIGH
        coeff = jnp.einsum(
            "prm,pmw->rw",
            gathered,
            table[1:].reshape(lon_groups, lon_cols, circle),
            precision=high,
        )
        coeff = jnp.where(wavenumber[None, :] <= limits[:, None], coeff * scale[None, :], 0.0)
        local_table = lax.dynamic_slice_in_dim(table, lon_index * lon_cols, lon_cols + 1, axis=0)
        lowpass_ext = jnp.einsum("rw,nw->rn", coeff, local_table, precision=high)
    else:
        whole_rows = jnp.transpose(gathered, (1, 0, 2)).reshape(flat_count, circle)
        lowpass = spectral_lowpass(whole_rows, limits, lon_groups)
        lowpass = jnp.concatenate([lowpass[:, -1:], lowpass], axis=1)
        lowpass_ext = lax.dynamic_slice_in_dim(lowpass, lon_index * lon_cols, lon_cols + 1, axis=1)
    filtered_flat = jnp.where((limits < circle // 2)[:, None], lowpass_ext, raw_ext)
    zonal_faces = filtered_flat.reshape(levels, 1, lat_rows, lon_cols + 1)
    filtered_zonal = zonal_faces[:, 0, :, 1:]
    flux_east = ppm_flux(lon_ext, zonal_faces, 3)
    face_weight, cell_weight = metric_weights(band_index * lat_rows, lat_rows, grid_rows)
    flux_north = (
        ppm_flux(lat_ext[:, :tracer_count], lat_ext[:, tracer_count:, 2 : lat_rows + 3, :], 2)
        * face_weight[None, None, :, None]
    )
    change = (
        flux_east[:, :, :, 1:]
        - flux_east[:, :, :, :-1]
        + (flux_north[:, :, 1:, :] - flux_north[:, :, :-1, :]) / cell_weight[None, None, :, None]
    )
    return (tracers - change, filtered_zonal)


def solution(mesh):
    in_specs = (P(None, None, "lat", "lon"), P(None, None, "lat", "lon"), P())
    out_specs = (P(None, None, "lat", "lon"), P(None, "lat", "lon"))
    return jax.shard_map(body, mesh=mesh, in_specs=in_specs, out_specs=out_specs, check_vma=False)
```

```python
import math

import jax
import numpy as np
import jax.numpy as jnp
from jax import lax
from jax.sharding import PartitionSpec as P


def padded(cells, sides, width, closed):
    for axis, dim in sides:
        count = lax.axis_size(axis)
        ends = count if closed else count - 1
        head = lax.slice_in_dim(cells, 0, width, axis=dim)
        tail = lax.slice_in_dim(cells, cells.shape[dim] - width, cells.shape[dim], axis=dim)
        cells = jnp.concatenate(
            [
                lax.ppermute(tail, axis, [(i, (i + 1) % count) for i in range(ends)]),
                cells,
                lax.ppermute(head, axis, [((i + 1) % count, i) for i in range(ends)]),
            ],
            axis=dim,
        )
    return cells


def take_range(values, start, count, axis_index):
    return lax.slice_in_dim(values, start, start + count, axis=axis_index)


def ppm_flux(extended, courant_faces, axis_index):
    cell_count = extended.shape[axis_index] - 6
    edge_values = 7.0 / 12.0 * (
        take_range(extended, 1, cell_count + 3, axis_index)
        + take_range(extended, 2, cell_count + 3, axis_index)
    ) - 1.0 / 12.0 * (
        take_range(extended, 0, cell_count + 3, axis_index)
        + take_range(extended, 3, cell_count + 3, axis_index)
    )
    left_edge = take_range(edge_values, 0, cell_count + 2, axis_index)
    right_edge = take_range(edge_values, 1, cell_count + 2, axis_index)
    centre = take_range(extended, 2, cell_count + 2, axis_index)
    slopes = right_edge - left_edge
    curvature = 6.0 * centre - 3.0 * (left_edge + right_edge)
    upwind = take_range(right_edge, 0, cell_count + 1, axis_index) - 0.5 * courant_faces * (
        take_range(slopes, 0, cell_count + 1, axis_index)
        - (1.0 - courant_faces * (2.0 / 3.0)) * take_range(curvature, 0, cell_count + 1, axis_index)
    )
    downwind = take_range(left_edge, 1, cell_count + 1, axis_index) - 0.5 * courant_faces * (
        take_range(slopes, 1, cell_count + 1, axis_index)
        + (1.0 + courant_faces * (2.0 / 3.0)) * take_range(curvature, 1, cell_count + 1, axis_index)
    )
    return courant_faces * jnp.where(courant_faces > 0, upwind, downwind)


def metric_weights(first_row, row_count, grid_rows):
    faces = first_row + jnp.arange(-1, row_count, dtype=jnp.int32)
    centres = first_row + jnp.arange(row_count, dtype=jnp.int32)
    face_weight = jnp.sin(
        jnp.minimum(faces + 1, grid_rows - 1 - faces).astype(jnp.float32) * (math.pi / grid_rows)
    )
    cell_weight = jnp.sin(
        (jnp.minimum(centres, grid_rows - 1 - centres).astype(jnp.float32) + 0.5)
        * (math.pi / grid_rows)
    )
    return (face_weight, cell_weight)


def angle_table(first_ids, second_ids, period):
    product = first_ids[:, None] * second_ids[None, :] % period
    angles = product.astype(jnp.float32) * (2.0 * math.pi / period)
    return (jnp.cos(angles), jnp.sin(angles))


def spectral_lowpass(row_block, limits, outer_count):
    row_count, circle = row_block.shape
    inner_count = circle // outer_count
    highest = lax.Precision.HIGHEST
    grid_values = row_block.reshape(row_count, outer_count, inner_count)
    outer_ids = jnp.arange(outer_count, dtype=jnp.int32)
    inner_ids = jnp.arange(inner_count, dtype=jnp.int32)
    outer_cos, outer_sin = angle_table(outer_ids, outer_ids, outer_count)
    inner_cos, inner_sin = angle_table(inner_ids, inner_ids, inner_count)
    twiddle_cos, twiddle_sin = angle_table(inner_ids, outer_ids, circle)
    first_real = jnp.einsum("rab,ak->rbk", grid_values, outer_cos, precision=highest)
    first_imag = -jnp.einsum("rab,ak->rbk", grid_values, outer_sin, precision=highest)
    turned_real = first_real * twiddle_cos + first_imag * twiddle_sin
    turned_imag = first_imag * twiddle_cos - first_real * twiddle_sin
    coeff_real = jnp.einsum("rbk,bj->rjk", turned_real, inner_cos, precision=highest) + jnp.einsum(
        "rbk,bj->rjk", turned_imag, inner_sin, precision=highest
    )
    coeff_imag = jnp.einsum("rbk,bj->rjk", turned_imag, inner_cos, precision=highest) - jnp.einsum(
        "rbk,bj->rjk", turned_real, inner_sin, precision=highest
    )
    wavenumber = inner_ids[:, None] * outer_count + outer_ids[None, :]
    folded = jnp.minimum(wavenumber, circle - wavenumber)
    keep_mask = folded[None, :, :] <= limits[:, None, None]
    coeff_real = jnp.where(keep_mask, coeff_real, 0.0)
    coeff_imag = jnp.where(keep_mask, coeff_imag, 0.0)
    back_real = jnp.einsum("rjk,jb->rbk", coeff_real, inner_cos, precision=highest) - jnp.einsum(
        "rjk,jb->rbk", coeff_imag, inner_sin, precision=highest
    )
    back_imag = jnp.einsum("rjk,jb->rbk", coeff_imag, inner_cos, precision=highest) + jnp.einsum(
        "rjk,jb->rbk", coeff_real, inner_sin, precision=highest
    )
    reverted_real = back_real * twiddle_cos - back_imag * twiddle_sin
    reverted_imag = back_imag * twiddle_cos + back_real * twiddle_sin
    signal = jnp.einsum("rbk,ka->rab", reverted_real, outer_cos, precision=highest) - jnp.einsum(
        "rbk,ka->rab", reverted_imag, outer_sin, precision=highest
    )
    return (signal / circle).reshape(row_count, circle)


def dense_tables(circle):
    half = circle // 2
    cell_ids = np.arange(-1, circle, dtype=np.int64)
    cos_ids = np.arange(half + 1, dtype=np.int64)
    sin_ids = np.arange(1, half, dtype=np.int64)
    table = np.concatenate(
        [
            np.cos(2.0 * np.pi * ((cell_ids[:, None] * cos_ids[None, :]) % circle) / circle),
            np.sin(2.0 * np.pi * ((cell_ids[:, None] * sin_ids[None, :]) % circle) / circle),
        ],
        axis=1,
    )
    wavenumber = np.concatenate([cos_ids, sin_ids])
    scale = np.where((wavenumber == 0) | (wavenumber == half), 1.0, 2.0) / circle
    return (table, scale, wavenumber)


def body(tracers, courant, cutoffs):
    levels, tracer_count, lat_rows, lon_cols = tracers.shape
    lon_groups = lax.axis_size("lon")
    lon_index = lax.axis_index("lon")
    lat_bands = lax.axis_size("lat")
    band_index = lax.axis_index("lat")
    grid_rows = lat_rows * lat_bands
    zonal = courant[0]
    meridional = courant[1]
    lat_stack = jnp.concatenate([tracers, meridional[:, None]], axis=1)
    lat_ext = padded(lat_stack, (("lat", 2),), 3, False)
    flat_count = levels * lat_rows
    flat_zonal = zonal.reshape(flat_count, lon_cols)
    edges = jnp.concatenate([tracers[..., :3], tracers[..., lon_cols - 3 :]], axis=-1)
    west_index = (lon_index + lon_groups - 1) % lon_groups
    east_index = (lon_index + 1) % lon_groups
    local_limits = lax.dynamic_slice_in_dim(cutoffs, band_index * lat_rows, lat_rows)
    limits = jnp.tile(local_limits, levels)
    circle = lon_cols * lon_groups
    if lon_groups <= 8 and circle <= 2048:
        edge_rows = jnp.transpose(edges, (0, 2, 1, 3)).reshape(flat_count, tracer_count * 6)
        payload = jnp.concatenate([flat_zonal, edge_rows], axis=1)
        received = [payload] + [
            lax.ppermute(payload, "lon", [(i, (i - s) % lon_groups) for i in range(lon_groups)])
            for s in range(1, lon_groups)
        ]

        def edge_block(part):
            block = part[:, lon_cols:].reshape(levels, lat_rows, tracer_count, 6)
            return jnp.transpose(block, (0, 2, 1, 3))

        east_part = received[1 % lon_groups]
        west_part = received[(lon_groups - 1) % lon_groups]
        west = edge_block(west_part)[..., 3:]
        east = edge_block(east_part)[..., :3]
        raw_ext = jnp.concatenate([west_part[:, lon_cols - 1 : lon_cols], flat_zonal], axis=1)
        table, scale, wavenumber = dense_tables(circle)
        width = payload.shape[1]
        forward = np.zeros((lon_groups, width, circle), np.float32)
        forward[:, :lon_cols, :] = table[1:].reshape(lon_groups, lon_cols, circle)
        forward = jnp.asarray(forward)
        inverse_rows = jnp.asarray(table[: lon_cols + 1].astype(np.float32))
        high = lax.Precision.HIGH
        coeff = jnp.dot(received[0], forward[0], precision=high)
        for s in range(1, lon_groups):
            coeff = coeff + jnp.dot(received[s], forward[s], precision=high)
        keep = jnp.asarray(wavenumber.astype(np.int32))[None, :] <= limits[:, None]
        coeff = jnp.where(keep, coeff * jnp.asarray(scale.astype(np.float32))[None, :], 0.0)
        lowpass_ext = jnp.einsum("rw,nw->rn", coeff, inverse_rows, precision=high)
    else:
        gathered = lax.all_gather(flat_zonal, "lon", axis=0)
        gathered_edges = lax.all_gather(edges, "lon", axis=0)
        west = lax.dynamic_index_in_dim(gathered_edges, west_index, 0, keepdims=False)[..., 3:]
        east = lax.dynamic_index_in_dim(gathered_edges, east_index, 0, keepdims=False)[..., :3]
        west_raw = lax.dynamic_index_in_dim(gathered, west_index, 0, keepdims=False)[:, -1:]
        raw_ext = jnp.concatenate([west_raw, flat_zonal], axis=1)
        whole_rows = jnp.transpose(gathered, (1, 0, 2)).reshape(flat_count, circle)
        lowpass = spectral_lowpass(whole_rows, limits, lon_groups)
        lowpass = jnp.concatenate([lowpass[:, -1:], lowpass], axis=1)
        lowpass_ext = lax.dynamic_slice_in_dim(lowpass, lon_index * lon_cols, lon_cols + 1, axis=1)
    lon_ext = jnp.concatenate([west, tracers, east], axis=-1)
    filtered_flat = jnp.where((limits < circle // 2)[:, None], lowpass_ext, raw_ext)
    zonal_faces = filtered_flat.reshape(levels, 1, lat_rows, lon_cols + 1)
    filtered_zonal = zonal_faces[:, 0, :, 1:]
    flux_east = ppm_flux(lon_ext, zonal_faces, 3)
    face_weight, cell_weight = metric_weights(band_index * lat_rows, lat_rows, grid_rows)
    flux_north = (
        ppm_flux(lat_ext[:, :tracer_count], lat_ext[:, tracer_count:, 2 : lat_rows + 3, :], 2)
        * face_weight[None, None, :, None]
    )
    change = (
        flux_east[:, :, :, 1:]
        - flux_east[:, :, :, :-1]
        + (flux_north[:, :, 1:, :] - flux_north[:, :, :-1, :]) / cell_weight[None, None, :, None]
    )
    return (tracers - change, filtered_zonal)


def solution(mesh):
    in_specs = (P(None, None, "lat", "lon"), P(None, None, "lat", "lon"), P())
    out_specs = (P(None, None, "lat", "lon"), P(None, "lat", "lon"))
    return jax.shard_map(body, mesh=mesh, in_specs=in_specs, out_specs=out_specs, check_vma=False)
```

```python
import math

import jax
import numpy as np
import jax.numpy as jnp
from jax import lax
from jax.sharding import PartitionSpec as P


def padded(cells, sides, width, closed):
    for axis, dim in sides:
        count = lax.axis_size(axis)
        ends = count if closed else count - 1
        head = lax.slice_in_dim(cells, 0, width, axis=dim)
        tail = lax.slice_in_dim(cells, cells.shape[dim] - width, cells.shape[dim], axis=dim)
        cells = jnp.concatenate(
            [
                lax.ppermute(tail, axis, [(i, (i + 1) % count) for i in range(ends)]),
                cells,
                lax.ppermute(head, axis, [((i + 1) % count, i) for i in range(ends)]),
            ],
            axis=dim,
        )
    return cells


def take_range(values, start, count, axis_index):
    return lax.slice_in_dim(values, start, start + count, axis=axis_index)


def ppm_flux(extended, courant_faces, axis_index):
    cell_count = extended.shape[axis_index] - 6
    edge_values = 7.0 / 12.0 * (
        take_range(extended, 1, cell_count + 3, axis_index)
        + take_range(extended, 2, cell_count + 3, axis_index)
    ) - 1.0 / 12.0 * (
        take_range(extended, 0, cell_count + 3, axis_index)
        + take_range(extended, 3, cell_count + 3, axis_index)
    )
    left_edge = take_range(edge_values, 0, cell_count + 2, axis_index)
    right_edge = take_range(edge_values, 1, cell_count + 2, axis_index)
    centre = take_range(extended, 2, cell_count + 2, axis_index)
    slopes = right_edge - left_edge
    curvature = 6.0 * centre - 3.0 * (left_edge + right_edge)
    upwind = take_range(right_edge, 0, cell_count + 1, axis_index) - 0.5 * courant_faces * (
        take_range(slopes, 0, cell_count + 1, axis_index)
        - (1.0 - courant_faces * (2.0 / 3.0)) * take_range(curvature, 0, cell_count + 1, axis_index)
    )
    downwind = take_range(left_edge, 1, cell_count + 1, axis_index) - 0.5 * courant_faces * (
        take_range(slopes, 1, cell_count + 1, axis_index)
        + (1.0 + courant_faces * (2.0 / 3.0)) * take_range(curvature, 1, cell_count + 1, axis_index)
    )
    return courant_faces * jnp.where(courant_faces > 0, upwind, downwind)


def metric_weights(first_row, row_count, grid_rows):
    faces = first_row + jnp.arange(-1, row_count, dtype=jnp.int32)
    centres = first_row + jnp.arange(row_count, dtype=jnp.int32)
    face_weight = jnp.sin(
        jnp.minimum(faces + 1, grid_rows - 1 - faces).astype(jnp.float32) * (math.pi / grid_rows)
    )
    cell_weight = jnp.sin(
        (jnp.minimum(centres, grid_rows - 1 - centres).astype(jnp.float32) + 0.5)
        * (math.pi / grid_rows)
    )
    return (face_weight, cell_weight)


def angle_table(first_ids, second_ids, period):
    product = first_ids[:, None] * second_ids[None, :] % period
    angles = product.astype(jnp.float32) * (2.0 * math.pi / period)
    return (jnp.cos(angles), jnp.sin(angles))


def spectral_lowpass(row_block, limits, outer_count):
    row_count, circle = row_block.shape
    inner_count = circle // outer_count
    highest = lax.Precision.HIGHEST
    grid_values = row_block.reshape(row_count, outer_count, inner_count)
    outer_ids = jnp.arange(outer_count, dtype=jnp.int32)
    inner_ids = jnp.arange(inner_count, dtype=jnp.int32)
    outer_cos, outer_sin = angle_table(outer_ids, outer_ids, outer_count)
    inner_cos, inner_sin = angle_table(inner_ids, inner_ids, inner_count)
    twiddle_cos, twiddle_sin = angle_table(inner_ids, outer_ids, circle)
    first_real = jnp.einsum("rab,ak->rbk", grid_values, outer_cos, precision=highest)
    first_imag = -jnp.einsum("rab,ak->rbk", grid_values, outer_sin, precision=highest)
    turned_real = first_real * twiddle_cos + first_imag * twiddle_sin
    turned_imag = first_imag * twiddle_cos - first_real * twiddle_sin
    coeff_real = jnp.einsum("rbk,bj->rjk", turned_real, inner_cos, precision=highest) + jnp.einsum(
        "rbk,bj->rjk", turned_imag, inner_sin, precision=highest
    )
    coeff_imag = jnp.einsum("rbk,bj->rjk", turned_imag, inner_cos, precision=highest) - jnp.einsum(
        "rbk,bj->rjk", turned_real, inner_sin, precision=highest
    )
    wavenumber = inner_ids[:, None] * outer_count + outer_ids[None, :]
    folded = jnp.minimum(wavenumber, circle - wavenumber)
    keep_mask = folded[None, :, :] <= limits[:, None, None]
    coeff_real = jnp.where(keep_mask, coeff_real, 0.0)
    coeff_imag = jnp.where(keep_mask, coeff_imag, 0.0)
    back_real = jnp.einsum("rjk,jb->rbk", coeff_real, inner_cos, precision=highest) - jnp.einsum(
        "rjk,jb->rbk", coeff_imag, inner_sin, precision=highest
    )
    back_imag = jnp.einsum("rjk,jb->rbk", coeff_imag, inner_cos, precision=highest) + jnp.einsum(
        "rjk,jb->rbk", coeff_real, inner_sin, precision=highest
    )
    reverted_real = back_real * twiddle_cos - back_imag * twiddle_sin
    reverted_imag = back_imag * twiddle_cos + back_real * twiddle_sin
    signal = jnp.einsum("rbk,ka->rab", reverted_real, outer_cos, precision=highest) - jnp.einsum(
        "rbk,ka->rab", reverted_imag, outer_sin, precision=highest
    )
    return (signal / circle).reshape(row_count, circle)


def dense_tables(circle):
    half = circle // 2
    cell_ids = np.arange(-1, circle, dtype=np.int64)
    cos_ids = np.arange(half + 1, dtype=np.int64)
    sin_ids = np.arange(1, half, dtype=np.int64)
    table = np.concatenate(
        [
            np.cos(2.0 * np.pi * ((cell_ids[:, None] * cos_ids[None, :]) % circle) / circle),
            np.sin(2.0 * np.pi * ((cell_ids[:, None] * sin_ids[None, :]) % circle) / circle),
        ],
        axis=1,
    )
    wavenumber = np.concatenate([cos_ids, sin_ids])
    scale = np.where((wavenumber == 0) | (wavenumber == half), 1.0, 2.0) / circle
    return (table, scale, wavenumber)


def body(tracers, courant, cutoffs):
    levels, tracer_count, lat_rows, lon_cols = tracers.shape
    lon_groups = lax.axis_size("lon")
    lon_index = lax.axis_index("lon")
    lat_bands = lax.axis_size("lat")
    band_index = lax.axis_index("lat")
    grid_rows = lat_rows * lat_bands
    zonal = courant[0]
    meridional = courant[1]
    lat_stack = jnp.concatenate([tracers, meridional[:, None]], axis=1)
    flat_count = levels * lat_rows
    flat_zonal = zonal.reshape(flat_count, lon_cols)
    edges = jnp.concatenate([tracers[..., :3], tracers[..., lon_cols - 3 :]], axis=-1)
    west_index = (lon_index + lon_groups - 1) % lon_groups
    east_index = (lon_index + 1) % lon_groups
    local_limits = lax.dynamic_slice_in_dim(cutoffs, band_index * lat_rows, lat_rows)
    limits = jnp.tile(local_limits, levels)
    circle = lon_cols * lon_groups
    if lon_groups <= 8 and circle <= 2048:
        edge_rows = jnp.transpose(edges, (0, 2, 1, 3)).reshape(flat_count, tracer_count * 6)
        payload = jnp.concatenate([flat_zonal, edge_rows], axis=1)
        received = [payload] + [
            lax.ppermute(payload, "lon", [(i, (i - s) % lon_groups) for i in range(lon_groups)])
            for s in range(1, lon_groups)
        ]

        lat_stack, received = lax.optimization_barrier((lat_stack, received))
        lat_ext = padded(lat_stack, (("lat", 2),), 3, False)

        def edge_block(part):
            block = part[:, lon_cols:].reshape(levels, lat_rows, tracer_count, 6)
            return jnp.transpose(block, (0, 2, 1, 3))

        east_part = received[1 % lon_groups]
        west_part = received[(lon_groups - 1) % lon_groups]
        west = edge_block(west_part)[..., 3:]
        east = edge_block(east_part)[..., :3]
        raw_ext = jnp.concatenate([west_part[:, lon_cols - 1 : lon_cols], flat_zonal], axis=1)
        table, scale, wavenumber = dense_tables(circle)
        width = payload.shape[1]
        forward = np.zeros((lon_groups, width, circle), np.float32)
        forward[:, :lon_cols, :] = table[1:].reshape(lon_groups, lon_cols, circle)
        forward = jnp.asarray(forward)
        inverse_rows = jnp.asarray(table[: lon_cols + 1].astype(np.float32))
        high = lax.Precision.HIGH
        coeff = jnp.dot(received[0], forward[0], precision=high)
        for s in range(1, lon_groups):
            coeff = coeff + jnp.dot(received[s], forward[s], precision=high)
        keep = jnp.asarray(wavenumber.astype(np.int32))[None, :] <= limits[:, None]
        coeff = jnp.where(keep, coeff * jnp.asarray(scale.astype(np.float32))[None, :], 0.0)
        lowpass_ext = jnp.einsum("rw,nw->rn", coeff, inverse_rows, precision=high)
    else:
        lat_ext = padded(lat_stack, (("lat", 2),), 3, False)
        gathered = lax.all_gather(flat_zonal, "lon", axis=0)
        gathered_edges = lax.all_gather(edges, "lon", axis=0)
        west = lax.dynamic_index_in_dim(gathered_edges, west_index, 0, keepdims=False)[..., 3:]
        east = lax.dynamic_index_in_dim(gathered_edges, east_index, 0, keepdims=False)[..., :3]
        west_raw = lax.dynamic_index_in_dim(gathered, west_index, 0, keepdims=False)[:, -1:]
        raw_ext = jnp.concatenate([west_raw, flat_zonal], axis=1)
        whole_rows = jnp.transpose(gathered, (1, 0, 2)).reshape(flat_count, circle)
        lowpass = spectral_lowpass(whole_rows, limits, lon_groups)
        lowpass = jnp.concatenate([lowpass[:, -1:], lowpass], axis=1)
        lowpass_ext = lax.dynamic_slice_in_dim(lowpass, lon_index * lon_cols, lon_cols + 1, axis=1)
    lon_ext = jnp.concatenate([west, tracers, east], axis=-1)
    filtered_flat = jnp.where((limits < circle // 2)[:, None], lowpass_ext, raw_ext)
    zonal_faces = filtered_flat.reshape(levels, 1, lat_rows, lon_cols + 1)
    filtered_zonal = zonal_faces[:, 0, :, 1:]
    flux_east = ppm_flux(lon_ext, zonal_faces, 3)
    face_weight, cell_weight = metric_weights(band_index * lat_rows, lat_rows, grid_rows)
    flux_north = (
        ppm_flux(lat_ext[:, :tracer_count], lat_ext[:, tracer_count:, 2 : lat_rows + 3, :], 2)
        * face_weight[None, None, :, None]
    )
    change = (
        flux_east[:, :, :, 1:]
        - flux_east[:, :, :, :-1]
        + (flux_north[:, :, 1:, :] - flux_north[:, :, :-1, :]) / cell_weight[None, None, :, None]
    )
    return (tracers - change, filtered_zonal)


def solution(mesh):
    in_specs = (P(None, None, "lat", "lon"), P(None, None, "lat", "lon"), P())
    out_specs = (P(None, None, "lat", "lon"), P(None, "lat", "lon"))
    return jax.shard_map(body, mesh=mesh, in_specs=in_specs, out_specs=out_specs, check_vma=False)
```

```python
import math

import jax
import numpy as np
import jax.numpy as jnp
from jax import lax
from jax.sharding import PartitionSpec as P


def padded(cells, sides, width, closed):
    for axis, dim in sides:
        count = lax.axis_size(axis)
        ends = count if closed else count - 1
        head = lax.slice_in_dim(cells, 0, width, axis=dim)
        tail = lax.slice_in_dim(cells, cells.shape[dim] - width, cells.shape[dim], axis=dim)
        cells = jnp.concatenate(
            [
                lax.ppermute(tail, axis, [(i, (i + 1) % count) for i in range(ends)]),
                cells,
                lax.ppermute(head, axis, [((i + 1) % count, i) for i in range(ends)]),
            ],
            axis=dim,
        )
    return cells


def take_range(values, start, count, axis_index):
    return lax.slice_in_dim(values, start, start + count, axis=axis_index)


def ppm_flux(extended, courant_faces, axis_index):
    cell_count = extended.shape[axis_index] - 6
    edge_values = 7.0 / 12.0 * (
        take_range(extended, 1, cell_count + 3, axis_index)
        + take_range(extended, 2, cell_count + 3, axis_index)
    ) - 1.0 / 12.0 * (
        take_range(extended, 0, cell_count + 3, axis_index)
        + take_range(extended, 3, cell_count + 3, axis_index)
    )
    left_edge = take_range(edge_values, 0, cell_count + 2, axis_index)
    right_edge = take_range(edge_values, 1, cell_count + 2, axis_index)
    centre = take_range(extended, 2, cell_count + 2, axis_index)
    slopes = right_edge - left_edge
    curvature = 6.0 * centre - 3.0 * (left_edge + right_edge)
    upwind = take_range(right_edge, 0, cell_count + 1, axis_index) - 0.5 * courant_faces * (
        take_range(slopes, 0, cell_count + 1, axis_index)
        - (1.0 - courant_faces * (2.0 / 3.0)) * take_range(curvature, 0, cell_count + 1, axis_index)
    )
    downwind = take_range(left_edge, 1, cell_count + 1, axis_index) - 0.5 * courant_faces * (
        take_range(slopes, 1, cell_count + 1, axis_index)
        + (1.0 + courant_faces * (2.0 / 3.0)) * take_range(curvature, 1, cell_count + 1, axis_index)
    )
    return courant_faces * jnp.where(courant_faces > 0, upwind, downwind)


def metric_weights(first_row, row_count, grid_rows):
    faces = first_row + jnp.arange(-1, row_count, dtype=jnp.int32)
    centres = first_row + jnp.arange(row_count, dtype=jnp.int32)
    face_weight = jnp.sin(
        jnp.minimum(faces + 1, grid_rows - 1 - faces).astype(jnp.float32) * (math.pi / grid_rows)
    )
    cell_weight = jnp.sin(
        (jnp.minimum(centres, grid_rows - 1 - centres).astype(jnp.float32) + 0.5)
        * (math.pi / grid_rows)
    )
    return (face_weight, cell_weight)


def angle_table(first_ids, second_ids, period):
    product = first_ids[:, None] * second_ids[None, :] % period
    angles = product.astype(jnp.float32) * (2.0 * math.pi / period)
    return (jnp.cos(angles), jnp.sin(angles))


def spectral_lowpass(row_block, limits, outer_count):
    row_count, circle = row_block.shape
    inner_count = circle // outer_count
    highest = lax.Precision.HIGHEST
    grid_values = row_block.reshape(row_count, outer_count, inner_count)
    outer_ids = jnp.arange(outer_count, dtype=jnp.int32)
    inner_ids = jnp.arange(inner_count, dtype=jnp.int32)
    outer_cos, outer_sin = angle_table(outer_ids, outer_ids, outer_count)
    inner_cos, inner_sin = angle_table(inner_ids, inner_ids, inner_count)
    twiddle_cos, twiddle_sin = angle_table(inner_ids, outer_ids, circle)
    first_real = jnp.einsum("rab,ak->rbk", grid_values, outer_cos, precision=highest)
    first_imag = -jnp.einsum("rab,ak->rbk", grid_values, outer_sin, precision=highest)
    turned_real = first_real * twiddle_cos + first_imag * twiddle_sin
    turned_imag = first_imag * twiddle_cos - first_real * twiddle_sin
    coeff_real = jnp.einsum("rbk,bj->rjk", turned_real, inner_cos, precision=highest) + jnp.einsum(
        "rbk,bj->rjk", turned_imag, inner_sin, precision=highest
    )
    coeff_imag = jnp.einsum("rbk,bj->rjk", turned_imag, inner_cos, precision=highest) - jnp.einsum(
        "rbk,bj->rjk", turned_real, inner_sin, precision=highest
    )
    wavenumber = inner_ids[:, None] * outer_count + outer_ids[None, :]
    folded = jnp.minimum(wavenumber, circle - wavenumber)
    keep_mask = folded[None, :, :] <= limits[:, None, None]
    coeff_real = jnp.where(keep_mask, coeff_real, 0.0)
    coeff_imag = jnp.where(keep_mask, coeff_imag, 0.0)
    back_real = jnp.einsum("rjk,jb->rbk", coeff_real, inner_cos, precision=highest) - jnp.einsum(
        "rjk,jb->rbk", coeff_imag, inner_sin, precision=highest
    )
    back_imag = jnp.einsum("rjk,jb->rbk", coeff_imag, inner_cos, precision=highest) + jnp.einsum(
        "rjk,jb->rbk", coeff_real, inner_sin, precision=highest
    )
    reverted_real = back_real * twiddle_cos - back_imag * twiddle_sin
    reverted_imag = back_imag * twiddle_cos + back_real * twiddle_sin
    signal = jnp.einsum("rbk,ka->rab", reverted_real, outer_cos, precision=highest) - jnp.einsum(
        "rbk,ka->rab", reverted_imag, outer_sin, precision=highest
    )
    return (signal / circle).reshape(row_count, circle)


def dense_tables(circle):
    half = circle // 2
    cell_ids = np.arange(-1, circle, dtype=np.int64)
    cos_ids = np.arange(half + 1, dtype=np.int64)
    sin_ids = np.arange(1, half, dtype=np.int64)
    table = np.concatenate(
        [
            np.cos(2.0 * np.pi * ((cell_ids[:, None] * cos_ids[None, :]) % circle) / circle),
            np.sin(2.0 * np.pi * ((cell_ids[:, None] * sin_ids[None, :]) % circle) / circle),
        ],
        axis=1,
    )
    wavenumber = np.concatenate([cos_ids, sin_ids])
    scale = np.where((wavenumber == 0) | (wavenumber == half), 1.0, 2.0) / circle
    return (table, scale, wavenumber)


def body(tracers, courant, cutoffs):
    levels, tracer_count, lat_rows, lon_cols = tracers.shape
    lon_groups = lax.axis_size("lon")
    lon_index = lax.axis_index("lon")
    lat_bands = lax.axis_size("lat")
    band_index = lax.axis_index("lat")
    grid_rows = lat_rows * lat_bands
    zonal = courant[0]
    meridional = courant[1]
    lat_count = lax.axis_size("lat")
    lat_head = jnp.concatenate([tracers[:, :, :3], meridional[:, None, :3]], axis=1)
    lat_tail = jnp.concatenate(
        [tracers[:, :, lat_rows - 3 :], meridional[:, None, lat_rows - 3 :]], axis=1
    )
    from_north = lax.ppermute(lat_tail, "lat", [(i, i + 1) for i in range(lat_count - 1)])
    from_south = lax.ppermute(lat_head, "lat", [(i + 1, i) for i in range(lat_count - 1)])
    lat_ext = jnp.concatenate(
        [from_north, jnp.concatenate([tracers, meridional[:, None]], axis=1), from_south], axis=2
    )
    flat_count = levels * lat_rows
    flat_zonal = zonal.reshape(flat_count, lon_cols)
    edges = jnp.concatenate([tracers[..., :3], tracers[..., lon_cols - 3 :]], axis=-1)
    west_index = (lon_index + lon_groups - 1) % lon_groups
    east_index = (lon_index + 1) % lon_groups
    local_limits = lax.dynamic_slice_in_dim(cutoffs, band_index * lat_rows, lat_rows)
    limits = jnp.tile(local_limits, levels)
    circle = lon_cols * lon_groups
    if lon_groups <= 8 and circle <= 2048:
        edge_rows = jnp.transpose(edges, (0, 2, 1, 3)).reshape(flat_count, tracer_count * 6)
        payload = jnp.concatenate([flat_zonal, edge_rows], axis=1)
        received = [payload] + [
            lax.ppermute(payload, "lon", [(i, (i - s) % lon_groups) for i in range(lon_groups)])
            for s in range(1, lon_groups)
        ]

        def edge_block(part):
            block = part[:, lon_cols:].reshape(levels, lat_rows, tracer_count, 6)
            return jnp.transpose(block, (0, 2, 1, 3))

        east_part = received[1 % lon_groups]
        west_part = received[(lon_groups - 1) % lon_groups]
        west = edge_block(west_part)[..., 3:]
        east = edge_block(east_part)[..., :3]
        raw_ext = jnp.concatenate([west_part[:, lon_cols - 1 : lon_cols], flat_zonal], axis=1)
        table, scale, wavenumber = dense_tables(circle)
        width = payload.shape[1]
        forward = np.zeros((lon_groups, width, circle), np.float32)
        forward[:, :lon_cols, :] = table[1:].reshape(lon_groups, lon_cols, circle)
        forward = jnp.asarray(forward)
        inverse_rows = jnp.asarray(table[: lon_cols + 1].astype(np.float32))
        high = lax.Precision.HIGH
        coeff = jnp.dot(received[0], forward[0], precision=high)
        for s in range(1, lon_groups):
            coeff = coeff + jnp.dot(received[s], forward[s], precision=high)
        keep = jnp.asarray(wavenumber.astype(np.int32))[None, :] <= limits[:, None]
        coeff = jnp.where(keep, coeff * jnp.asarray(scale.astype(np.float32))[None, :], 0.0)
        lowpass_ext = jnp.einsum("rw,nw->rn", coeff, inverse_rows, precision=high)
    else:
        gathered = lax.all_gather(flat_zonal, "lon", axis=0)
        gathered_edges = lax.all_gather(edges, "lon", axis=0)
        west = lax.dynamic_index_in_dim(gathered_edges, west_index, 0, keepdims=False)[..., 3:]
        east = lax.dynamic_index_in_dim(gathered_edges, east_index, 0, keepdims=False)[..., :3]
        west_raw = lax.dynamic_index_in_dim(gathered, west_index, 0, keepdims=False)[:, -1:]
        raw_ext = jnp.concatenate([west_raw, flat_zonal], axis=1)
        whole_rows = jnp.transpose(gathered, (1, 0, 2)).reshape(flat_count, circle)
        lowpass = spectral_lowpass(whole_rows, limits, lon_groups)
        lowpass = jnp.concatenate([lowpass[:, -1:], lowpass], axis=1)
        lowpass_ext = lax.dynamic_slice_in_dim(lowpass, lon_index * lon_cols, lon_cols + 1, axis=1)
    lon_ext = jnp.concatenate([west, tracers, east], axis=-1)
    filtered_flat = jnp.where((limits < circle // 2)[:, None], lowpass_ext, raw_ext)
    zonal_faces = filtered_flat.reshape(levels, 1, lat_rows, lon_cols + 1)
    filtered_zonal = zonal_faces[:, 0, :, 1:]
    flux_east = ppm_flux(lon_ext, zonal_faces, 3)
    face_weight, cell_weight = metric_weights(band_index * lat_rows, lat_rows, grid_rows)
    flux_north = (
        ppm_flux(lat_ext[:, :tracer_count], lat_ext[:, tracer_count:, 2 : lat_rows + 3, :], 2)
        * face_weight[None, None, :, None]
    )
    change = (
        flux_east[:, :, :, 1:]
        - flux_east[:, :, :, :-1]
        + (flux_north[:, :, 1:, :] - flux_north[:, :, :-1, :]) / cell_weight[None, None, :, None]
    )
    return (tracers - change, filtered_zonal)


def solution(mesh):
    in_specs = (P(None, None, "lat", "lon"), P(None, None, "lat", "lon"), P())
    out_specs = (P(None, None, "lat", "lon"), P(None, "lat", "lon"))
    return jax.shard_map(body, mesh=mesh, in_specs=in_specs, out_specs=out_specs, check_vma=False)
```

```python
import math

import jax
import numpy as np
import jax.numpy as jnp
from jax import lax
from jax.sharding import PartitionSpec as P


def padded(cells, sides, width, closed):
    for axis, dim in sides:
        count = lax.axis_size(axis)
        ends = count if closed else count - 1
        head = lax.slice_in_dim(cells, 0, width, axis=dim)
        tail = lax.slice_in_dim(cells, cells.shape[dim] - width, cells.shape[dim], axis=dim)
        cells = jnp.concatenate(
            [
                lax.ppermute(tail, axis, [(i, (i + 1) % count) for i in range(ends)]),
                cells,
                lax.ppermute(head, axis, [((i + 1) % count, i) for i in range(ends)]),
            ],
            axis=dim,
        )
    return cells


def take_range(values, start, count, axis_index):
    return lax.slice_in_dim(values, start, start + count, axis=axis_index)


def ppm_flux(extended, courant_faces, axis_index):
    cell_count = extended.shape[axis_index] - 6
    edge_values = 7.0 / 12.0 * (
        take_range(extended, 1, cell_count + 3, axis_index)
        + take_range(extended, 2, cell_count + 3, axis_index)
    ) - 1.0 / 12.0 * (
        take_range(extended, 0, cell_count + 3, axis_index)
        + take_range(extended, 3, cell_count + 3, axis_index)
    )
    left_edge = take_range(edge_values, 0, cell_count + 2, axis_index)
    right_edge = take_range(edge_values, 1, cell_count + 2, axis_index)
    centre = take_range(extended, 2, cell_count + 2, axis_index)
    slopes = right_edge - left_edge
    curvature = 6.0 * centre - 3.0 * (left_edge + right_edge)
    upwind = take_range(right_edge, 0, cell_count + 1, axis_index) - 0.5 * courant_faces * (
        take_range(slopes, 0, cell_count + 1, axis_index)
        - (1.0 - courant_faces * (2.0 / 3.0)) * take_range(curvature, 0, cell_count + 1, axis_index)
    )
    downwind = take_range(left_edge, 1, cell_count + 1, axis_index) - 0.5 * courant_faces * (
        take_range(slopes, 1, cell_count + 1, axis_index)
        + (1.0 + courant_faces * (2.0 / 3.0)) * take_range(curvature, 1, cell_count + 1, axis_index)
    )
    return courant_faces * jnp.where(courant_faces > 0, upwind, downwind)


def metric_weights(first_row, row_count, grid_rows):
    faces = first_row + jnp.arange(-1, row_count, dtype=jnp.int32)
    centres = first_row + jnp.arange(row_count, dtype=jnp.int32)
    face_weight = jnp.sin(
        jnp.minimum(faces + 1, grid_rows - 1 - faces).astype(jnp.float32) * (math.pi / grid_rows)
    )
    cell_weight = jnp.sin(
        (jnp.minimum(centres, grid_rows - 1 - centres).astype(jnp.float32) + 0.5)
        * (math.pi / grid_rows)
    )
    return (face_weight, cell_weight)


def angle_table(first_ids, second_ids, period):
    product = first_ids[:, None] * second_ids[None, :] % period
    angles = product.astype(jnp.float32) * (2.0 * math.pi / period)
    return (jnp.cos(angles), jnp.sin(angles))


def spectral_lowpass(row_block, limits, outer_count):
    row_count, circle = row_block.shape
    inner_count = circle // outer_count
    highest = lax.Precision.HIGHEST
    grid_values = row_block.reshape(row_count, outer_count, inner_count)
    outer_ids = jnp.arange(outer_count, dtype=jnp.int32)
    inner_ids = jnp.arange(inner_count, dtype=jnp.int32)
    outer_cos, outer_sin = angle_table(outer_ids, outer_ids, outer_count)
    inner_cos, inner_sin = angle_table(inner_ids, inner_ids, inner_count)
    twiddle_cos, twiddle_sin = angle_table(inner_ids, outer_ids, circle)
    first_real = jnp.einsum("rab,ak->rbk", grid_values, outer_cos, precision=highest)
    first_imag = -jnp.einsum("rab,ak->rbk", grid_values, outer_sin, precision=highest)
    turned_real = first_real * twiddle_cos + first_imag * twiddle_sin
    turned_imag = first_imag * twiddle_cos - first_real * twiddle_sin
    coeff_real = jnp.einsum("rbk,bj->rjk", turned_real, inner_cos, precision=highest) + jnp.einsum(
        "rbk,bj->rjk", turned_imag, inner_sin, precision=highest
    )
    coeff_imag = jnp.einsum("rbk,bj->rjk", turned_imag, inner_cos, precision=highest) - jnp.einsum(
        "rbk,bj->rjk", turned_real, inner_sin, precision=highest
    )
    wavenumber = inner_ids[:, None] * outer_count + outer_ids[None, :]
    folded = jnp.minimum(wavenumber, circle - wavenumber)
    keep_mask = folded[None, :, :] <= limits[:, None, None]
    coeff_real = jnp.where(keep_mask, coeff_real, 0.0)
    coeff_imag = jnp.where(keep_mask, coeff_imag, 0.0)
    back_real = jnp.einsum("rjk,jb->rbk", coeff_real, inner_cos, precision=highest) - jnp.einsum(
        "rjk,jb->rbk", coeff_imag, inner_sin, precision=highest
    )
    back_imag = jnp.einsum("rjk,jb->rbk", coeff_imag, inner_cos, precision=highest) + jnp.einsum(
        "rjk,jb->rbk", coeff_real, inner_sin, precision=highest
    )
    reverted_real = back_real * twiddle_cos - back_imag * twiddle_sin
    reverted_imag = back_imag * twiddle_cos + back_real * twiddle_sin
    signal = jnp.einsum("rbk,ka->rab", reverted_real, outer_cos, precision=highest) - jnp.einsum(
        "rbk,ka->rab", reverted_imag, outer_sin, precision=highest
    )
    return (signal / circle).reshape(row_count, circle)


def dense_tables(circle):
    half = circle // 2
    cell_ids = np.arange(-1, circle, dtype=np.int64)
    cos_ids = np.arange(half + 1, dtype=np.int64)
    sin_ids = np.arange(1, half, dtype=np.int64)
    table = np.concatenate(
        [
            np.cos(2.0 * np.pi * ((cell_ids[:, None] * cos_ids[None, :]) % circle) / circle),
            np.sin(2.0 * np.pi * ((cell_ids[:, None] * sin_ids[None, :]) % circle) / circle),
        ],
        axis=1,
    )
    wavenumber = np.concatenate([cos_ids, sin_ids])
    scale = np.where((wavenumber == 0) | (wavenumber == half), 1.0, 2.0) / circle
    return (table, scale, wavenumber)


def body(tracers, courant, cutoffs):
    levels, tracer_count, lat_rows, lon_cols = tracers.shape
    lon_groups = lax.axis_size("lon")
    lon_index = lax.axis_index("lon")
    lat_bands = lax.axis_size("lat")
    band_index = lax.axis_index("lat")
    grid_rows = lat_rows * lat_bands
    zonal = courant[0]
    meridional = courant[1]
    lat_count = lax.axis_size("lat")
    lat_head = tracers[:, :, :3]
    lat_tail = jnp.concatenate(
        [tracers[:, :, lat_rows - 3 :], meridional[:, None, lat_rows - 3 :]], axis=1
    )
    from_north = lax.ppermute(lat_tail, "lat", [(i, i + 1) for i in range(lat_count - 1)])
    from_south = lax.ppermute(lat_head, "lat", [(i + 1, i) for i in range(lat_count - 1)])
    lat_ext = jnp.concatenate([from_north[:, :tracer_count], tracers, from_south], axis=2)
    north_faces = jnp.concatenate([from_north[:, tracer_count:, 2:], meridional[:, None]], axis=2)
    flat_count = levels * lat_rows
    flat_zonal = zonal.reshape(flat_count, lon_cols)
    edges = jnp.concatenate([tracers[..., :3], tracers[..., lon_cols - 3 :]], axis=-1)
    west_index = (lon_index + lon_groups - 1) % lon_groups
    east_index = (lon_index + 1) % lon_groups
    local_limits = lax.dynamic_slice_in_dim(cutoffs, band_index * lat_rows, lat_rows)
    limits = jnp.tile(local_limits, levels)
    circle = lon_cols * lon_groups
    if lon_groups <= 8 and circle <= 2048:
        edge_rows = jnp.transpose(edges, (0, 2, 1, 3)).reshape(flat_count, tracer_count * 6)
        payload = jnp.concatenate([flat_zonal, edge_rows], axis=1)
        received = [payload] + [
            lax.ppermute(payload, "lon", [(i, (i - s) % lon_groups) for i in range(lon_groups)])
            for s in range(1, lon_groups)
        ]

        def edge_block(part):
            block = part[:, lon_cols:].reshape(levels, lat_rows, tracer_count, 6)
            return jnp.transpose(block, (0, 2, 1, 3))

        east_part = received[1 % lon_groups]
        west_part = received[(lon_groups - 1) % lon_groups]
        west = edge_block(west_part)[..., 3:]
        east = edge_block(east_part)[..., :3]
        raw_ext = jnp.concatenate([west_part[:, lon_cols - 1 : lon_cols], flat_zonal], axis=1)
        table, scale, wavenumber = dense_tables(circle)
        width = payload.shape[1]
        forward = np.zeros((lon_groups, width, circle), np.float32)
        forward[:, :lon_cols, :] = table[1:].reshape(lon_groups, lon_cols, circle)
        forward = jnp.asarray(forward)
        inverse_rows = jnp.asarray(table[: lon_cols + 1].astype(np.float32))
        high = lax.Precision.HIGH
        coeff = jnp.dot(received[0], forward[0], precision=high)
        for s in range(1, lon_groups):
            coeff = coeff + jnp.dot(received[s], forward[s], precision=high)
        keep = jnp.asarray(wavenumber.astype(np.int32))[None, :] <= limits[:, None]
        coeff = jnp.where(keep, coeff * jnp.asarray(scale.astype(np.float32))[None, :], 0.0)
        lowpass_ext = jnp.einsum("rw,nw->rn", coeff, inverse_rows, precision=high)
    else:
        gathered = lax.all_gather(flat_zonal, "lon", axis=0)
        gathered_edges = lax.all_gather(edges, "lon", axis=0)
        west = lax.dynamic_index_in_dim(gathered_edges, west_index, 0, keepdims=False)[..., 3:]
        east = lax.dynamic_index_in_dim(gathered_edges, east_index, 0, keepdims=False)[..., :3]
        west_raw = lax.dynamic_index_in_dim(gathered, west_index, 0, keepdims=False)[:, -1:]
        raw_ext = jnp.concatenate([west_raw, flat_zonal], axis=1)
        whole_rows = jnp.transpose(gathered, (1, 0, 2)).reshape(flat_count, circle)
        lowpass = spectral_lowpass(whole_rows, limits, lon_groups)
        lowpass = jnp.concatenate([lowpass[:, -1:], lowpass], axis=1)
        lowpass_ext = lax.dynamic_slice_in_dim(lowpass, lon_index * lon_cols, lon_cols + 1, axis=1)
    lon_ext = jnp.concatenate([west, tracers, east], axis=-1)
    filtered_flat = jnp.where((limits < circle // 2)[:, None], lowpass_ext, raw_ext)
    zonal_faces = filtered_flat.reshape(levels, 1, lat_rows, lon_cols + 1)
    filtered_zonal = zonal_faces[:, 0, :, 1:]
    flux_east = ppm_flux(lon_ext, zonal_faces, 3)
    face_weight, cell_weight = metric_weights(band_index * lat_rows, lat_rows, grid_rows)
    flux_north = (
        ppm_flux(lat_ext, north_faces, 2)
        * face_weight[None, None, :, None]
    )
    change = (
        flux_east[:, :, :, 1:]
        - flux_east[:, :, :, :-1]
        + (flux_north[:, :, 1:, :] - flux_north[:, :, :-1, :]) / cell_weight[None, None, :, None]
    )
    return (tracers - change, filtered_zonal)


def solution(mesh):
    in_specs = (P(None, None, "lat", "lon"), P(None, None, "lat", "lon"), P())
    out_specs = (P(None, None, "lat", "lon"), P(None, "lat", "lon"))
    return jax.shard_map(body, mesh=mesh, in_specs=in_specs, out_specs=out_specs, check_vma=False)
```
